32 devices in a mesh: rep: 8 (over z, core), rows: 4 (over y, x).
Axes of the slice: x: 2, y: 2, z: 4, core: 2. Of those that a mesh axis runs over, the one named last changes fastest.
Arguments:
- weights: bfloat16 [7168, 2048], P('rows'), may hold values from -6 to 6
- momentum: float32 [8, 7168, 2048], P('rep', 'rows'), may hold values from -8 to 8
- gradient: bfloat16 [8, 7168, 2048], P('rep', 'rows'), may hold values from -8 to 8
- right_factor: float32 [2048, 512], P('rows'), may hold values from -6 to 6
Outputs:
- new_weights: bfloat16 [7168, 2048], P('rows')
- new_momentum: float32 [8, 7168, 2048], P('rep', 'rows')
- new_right: float32 [2048, 512], P('rows')
The draws below stay inside these ranges and needn't reach their ends.
All inputs are finite; a program needn't handle non-finite values.
Results may differ from the reference program's by a relative error of at most 0.019.
Values may be sent and summed in bfloat16 or wider, within the bound.
A program may use at most 128 MiB of HBM per device.

```python
import math
import jax
import jax.numpy as jnp
from jax import lax

M = 7168
N = 2048
RANK = 512
GROUPS = 8


def shared_signal(key):
    rank_part = RANK // 2
    left_part = jax.random.normal(jax.random.fold_in(key, 101), (M, rank_part), jnp.float32)
    right_part = jax.random.normal(jax.random.fold_in(key, 202), (rank_part, N), jnp.float32)
    signal = jnp.dot(left_part, right_part, precision=lax.Precision.HIGHEST) / math.sqrt(rank_part)
    return signal


def noise_of(key, offset_key):
    sub_key = jax.random.fold_in(key, offset_key)
    return 0.5 * jax.random.normal(sub_key, (GROUPS, M, N), jnp.float32)


def draw_momentum(key, part):
    signal = shared_signal(key)
    values = 0.6 * signal[None] + noise_of(key, 11)
    return jnp.clip(values, -8.0, 8.0).astype(jnp.float32)


def draw_gradient(key, part):
    signal = shared_signal(key)
    values = 0.2 * signal[None] + noise_of(key, 12)
    return jnp.clip(values, -8.0, 8.0).astype(jnp.bfloat16)


def steps_of(key, extent, shards, least, largest):
    gain, own = 1.0, jax.random.fold_in(key, 6)
    for axis_at, shards_of in shards:
        steps = jnp.exp(jax.random.uniform(jax.random.fold_in(own, axis_at), (shards_of,), jnp.float32, least / len(shards), largest / len(shards)))
        gain = gain * jnp.repeat(steps, extent[axis_at] // shards_of).reshape([-1 if axis == axis_at else 1 for axis in range(len(extent))])
    return gain


def gaussian(key, extent, spread, most, shards=(), kind=jnp.bfloat16):
    array = jax.random.normal(key, extent, jnp.float32) * spread
    if len(shards) > 0:
        array = steps_of(key, extent, shards, -0.22, 0.18) * array
    return jnp.clip(array, min=-most, max=most).astype(kind)


def setup_inputs(seed: int = 0) -> dict:
    seeds = jax.random.split(jax.random.key(seed), 5)
    weights = gaussian(seeds[0], (M, N), 1.0, 6.0, ((0, 4),))
    momentum = draw_momentum(jax.random.fold_in(seeds[4], 71), 0)
    gradient = draw_gradient(jax.random.fold_in(seeds[4], 71), 0)
    right_factor = gaussian(seeds[3], (N, RANK), 1.0, 6.0, ((0, 4),), jnp.float32)
    return dict(weights=weights, momentum=momentum, gradient=gradient, right_factor=right_factor)


momentum_keep = 0.05
learn_rate = 0.5
tiny = 1e-06

def reference(weights, momentum, gradient, right_factor):
    right_half = right_factor.astype(jnp.bfloat16)

    def left_of(pair):
        mom, grad = pair
        combined_half = (mom + grad.astype(jnp.float32)).astype(jnp.bfloat16)
        left = jnp.dot(combined_half.astype(jnp.float32), right_half.astype(jnp.float32), preferred_element_type=jnp.float32).astype(jnp.bfloat16)
        return lax.optimization_barrier(left).astype(jnp.float32)
    left_each = lax.map(left_of, (momentum, gradient))
    left_mean = lax.optimization_barrier(jnp.sum(left_each, 0)) / GROUPS
    gram = jnp.dot(left_mean.T, left_mean, precision=lax.Precision.HIGHEST)
    chol = jnp.linalg.cholesky(gram)
    left_orth = jax.scipy.linalg.solve_triangular(chol, left_mean.T, lower=True).T
    left_half = left_orth.astype(jnp.bfloat16)

    def right_of(pair):
        mom, grad = pair
        combined_half = (mom + grad.astype(jnp.float32)).astype(jnp.bfloat16)
        return jnp.dot(combined_half.T.astype(jnp.float32), left_half.astype(jnp.float32), preferred_element_type=jnp.float32)
    right_mean = lax.optimization_barrier(jnp.sum(lax.map(right_of, (momentum, gradient)), 0)) / GROUPS
    feedback = jnp.dot(left_half.astype(jnp.float32), right_mean.astype(jnp.bfloat16).T.astype(jnp.float32), preferred_element_type=jnp.float32)

    def moment_of(pair):
        mom, grad = pair
        return mom + grad.astype(jnp.float32) - momentum_keep * feedback
    new_momentum = lax.map(moment_of, (momentum, gradient))
    new_right = right_mean / jnp.sqrt(lax.optimization_barrier(jnp.mean(right_mean * right_mean, axis=0)) + tiny)
    update = jnp.dot(left_half.astype(jnp.float32), new_right.astype(jnp.bfloat16).T.astype(jnp.float32), preferred_element_type=jnp.float32)
    new_weights = (weights.astype(jnp.float32) - learn_rate * jnp.sqrt(M / N) * update).astype(jnp.bfloat16)
    return (new_weights, new_momentum, new_right)
```

```python
import jax, jax.numpy as jnp
from jax import lax
from jax.experimental import pallas as pl
from jax.experimental.pallas import tpu as pltpu
from jax.sharding import PartitionSpec as P

M = 7168
N = 2048


momentum_keep = 0.05
learn_rate = 0.5
tiny = 1e-06


HI = lax.Precision.HIGHEST
F32 = jnp.float32

def dot_tn(a, b):
    return lax.dot_general(a, b, (((0,), (0,)), ((), ())), precision=HI, preferred_element_type=F32)

def factor_block(work, size, step):
    wide = 2 * size
    for at in range(0, size, step):
        panel = work[at:at + step, :]
        el = {}
        for i in range(step):
            for k in range(i + 1):
                el[i, k] = jnp.broadcast_to(panel[k:k + 1, at + i:at + i + 1], (1, size))
        rows = [(panel[i:i + 1, :size], panel[i:i + 1, size:]) for i in range(step)]
        done = []
        for k in range(step):
            inv = lax.rsqrt(el[k, k])
            own = (rows[k][0] * inv, rows[k][1] * inv)
            done.append(own)
            col = {i: el[i, k] * inv for i in range(k + 1, step)}
            for i in range(k + 1, step):
                rows[i] = (rows[i][0] - col[i] * own[0], rows[i][1] - col[i] * own[1])
                for m in range(k + 1, i + 1):
                    el[i, m] = el[i, m] - col[i] * col[m]
        upper = jnp.concatenate([d[0] for d in done], axis=0)
        aug = jnp.concatenate([d[1] for d in done], axis=0)
        work[at:at + step, :size] = upper
        work[at:at + step, size:] = aug
        nxt = at + step
        if nxt < size:
            upd = dot_tn(upper, jnp.concatenate([upper, aug], axis=1))
            work[nxt:, :] = work[nxt:, :] - upd[nxt:, :]

def chol_kernel(size, step, gram_ref, out_ref, full, work):
    rank = gram_ref.shape[0]
    full[:, :rank] = gram_ref[...]
    r = lax.broadcasted_iota(jnp.int32, (rank, rank), 0)
    c = lax.broadcasted_iota(jnp.int32, (rank, rank), 1)
    full[:, rank:] = jnp.where(r == c, 1.0, 0.0).astype(F32)
    rb = lax.broadcasted_iota(jnp.int32, (size, size), 0)
    cb = lax.broadcasted_iota(jnp.int32, (size, size), 1)
    eye = jnp.where(rb == cb, 1.0, 0.0).astype(F32)
    for at in range(0, rank, size):
        work[:, :size] = full[at:at + size, at:at + size]
        work[:, size:] = eye
        factor_block(work, size, step)
        inv = jnp.where(rb >= cb, work[:, size:], 0.0)
        block = jnp.dot(inv, full[at:at + size, :], precision=HI, preferred_element_type=F32)
        out_ref[at:at + size, :] = block[:, rank:]
        nxt = at + size
        if nxt < rank:
            full[nxt:, :] = full[nxt:, :] - dot_tn(block[:, nxt:rank], block)

def inverse_factor(gram):
    rank = gram.shape[0]
    size = 128
    return pl.pallas_call(
        lambda *refs: chol_kernel(size, 8, *refs),
        out_shape=jax.ShapeDtypeStruct((rank, rank), F32),
        in_specs=[pl.BlockSpec(memory_space=pltpu.VMEM)],
        out_specs=pl.BlockSpec(memory_space=pltpu.VMEM),
        scratch_shapes=[pltpu.VMEM((rank, 2 * rank), F32), pltpu.VMEM((size, 2 * size), F32)],
        name="inverse_factor",
    )(gram)


def per_device(weights, momentum, gradient, right_factor):
    groups = lax.axis_size("rep")
    shards = lax.axis_size("rows")
    combined = momentum[0] + gradient[0].astype(jnp.float32)
    combined_half = combined.astype(jnp.bfloat16)
    columns = combined.shape[1]
    share = columns // shards
    left_local = jnp.dot(
        combined_half,
        lax.all_gather(right_factor.astype(jnp.bfloat16), "rows", axis=0, tiled=True),
        preferred_element_type=jnp.float32,
    )
    left_local = lax.optimization_barrier(left_local.astype(jnp.bfloat16)).astype(jnp.float32)
    left_mean = lax.psum(left_local.astype(jnp.bfloat16), "rep").astype(jnp.float32) / groups
    gram = lax.psum(jnp.dot(left_mean.T, left_mean, precision=lax.Precision.HIGHEST), "rows")
    inverse = inverse_factor(gram)
    left_orth = jnp.dot(left_mean, inverse.T, precision=lax.Precision.HIGHEST)
    left_half = left_orth.astype(jnp.bfloat16)
    partial_right = jnp.einsum(
        "ij,ik->jk", combined_half, left_half, preferred_element_type=jnp.float32
    )
    right_mean = lax.psum(partial_right, ("rep", "rows")) / groups
    normed = right_mean / jnp.sqrt(jnp.mean(right_mean * right_mean, axis=0) + tiny)
    feedback = jnp.dot(
        left_half, right_mean.astype(jnp.bfloat16).T, preferred_element_type=jnp.float32
    )
    update = jnp.dot(left_half, normed.astype(jnp.bfloat16).T, preferred_element_type=jnp.float32)
    new_right = lax.dynamic_slice_in_dim(normed, lax.axis_index("rows") * share, share, 0)
    new_momentum = combined - momentum_keep * feedback
    new_weights = (weights.astype(jnp.float32) - learn_rate * jnp.sqrt(M / N) * update).astype(
        jnp.bfloat16
    )
    return (new_weights, new_momentum[None], new_right)


def solution(mesh):
    in_specs = (P("rows", None), P("rep", "rows", None), P("rep", "rows", None), P("rows", None))
    out_specs = (P("rows", None), P("rep", "rows", None), P("rows", None))
    return jax.shard_map(
        per_device, mesh=mesh, in_specs=in_specs, out_specs=out_specs, check_vma=False
    )
```

```python
import functools

import jax, jax.numpy as jnp
from jax import lax
from jax.experimental import pallas as pl
from jax.experimental.pallas import tpu as pltpu
from jax.sharding import PartitionSpec as P

M = 7168
N = 2048


momentum_keep = 0.05
learn_rate = 0.5
tiny = 1e-06


HI = lax.Precision.HIGHEST
F32 = jnp.float32

def dot_tn(a, b):
    return lax.dot_general(a, b, (((0,), (0,)), ((), ())), precision=HI, preferred_element_type=F32)

def factor_block(work, size, step):
    wide = 2 * size
    for at in range(0, size, step):
        panel = work[at:at + step, :]
        el = {}
        for i in range(step):
            for k in range(i + 1):
                el[i, k] = jnp.broadcast_to(panel[k:k + 1, at + i:at + i + 1], (1, size))
        rows = [(panel[i:i + 1, :size], panel[i:i + 1, size:]) for i in range(step)]
        done = []
        for k in range(step):
            inv = lax.rsqrt(el[k, k])
            own = (rows[k][0] * inv, rows[k][1] * inv)
            done.append(own)
            col = {i: el[i, k] * inv for i in range(k + 1, step)}
            for i in range(k + 1, step):
                rows[i] = (rows[i][0] - col[i] * own[0], rows[i][1] - col[i] * own[1])
                for m in range(k + 1, i + 1):
                    el[i, m] = el[i, m] - col[i] * col[m]
        upper = jnp.concatenate([d[0] for d in done], axis=0)
        aug = jnp.concatenate([d[1] for d in done], axis=0)
        work[at:at + step, :size] = upper
        work[at:at + step, size:] = aug
        nxt = at + step
        if nxt < size:
            upd = dot_tn(upper, jnp.concatenate([upper, aug], axis=1))
            work[nxt:, :] = work[nxt:, :] - upd[nxt:, :]

def chol_kernel(size, step, gram_ref, out_ref, full, work):
    rank = gram_ref.shape[0]
    full[:, :rank] = gram_ref[...]
    r = lax.broadcasted_iota(jnp.int32, (rank, rank), 0)
    c = lax.broadcasted_iota(jnp.int32, (rank, rank), 1)
    full[:, rank:] = jnp.where(r == c, 1.0, 0.0).astype(F32)
    rb = lax.broadcasted_iota(jnp.int32, (size, size), 0)
    cb = lax.broadcasted_iota(jnp.int32, (size, size), 1)
    eye = jnp.where(rb == cb, 1.0, 0.0).astype(F32)
    for at in range(0, rank, size):
        work[:, :size] = full[at:at + size, at:at + size]
        work[:, size:] = eye
        factor_block(work, size, step)
        inv = jnp.where(rb >= cb, work[:, size:], 0.0)
        block = jnp.dot(inv, full[at:at + size, :], precision=HI, preferred_element_type=F32)
        out_ref[at:at + size, :] = block[:, rank:]
        nxt = at + size
        if nxt < rank:
            full[nxt:, :] = full[nxt:, :] - dot_tn(block[:, nxt:rank], block)

def inverse_factor(gram):
    rank = gram.shape[0]
    size = 128
    return pl.pallas_call(
        lambda *refs: chol_kernel(size, 8, *refs),
        out_shape=jax.ShapeDtypeStruct((rank, rank), F32),
        in_specs=[pl.BlockSpec(memory_space=pltpu.VMEM)],
        out_specs=pl.BlockSpec(memory_space=pltpu.VMEM),
        scratch_shapes=[pltpu.VMEM((rank, 2 * rank), F32), pltpu.VMEM((size, 2 * size), F32)],
        name="inverse_factor",
    )(gram)


MESH = pl.DeviceIdType.MESH
BF16 = jnp.bfloat16


class Net:
    def __init__(self, parts, shards):
        self.P, self.R, self.Z = parts, shards, parts // 2
        self.r, self.j = lax.axis_index("rep"), lax.axis_index("rows")
        self.z, self.c = self.r // 2, lax.rem(self.r, 2)
        self.other = 1 - self.c
        self.partner = (2 * self.z + self.other, self.j)

    def row(self, step):
        return lax.rem(self.j + step + self.R, self.R)

    def level(self, step):
        return lax.rem(self.z + step + self.Z, self.Z)

    def row_peer(self, step):
        return (self.r, self.row(step))

    def level_peer(self, step):
        return (2 * self.level(step) + self.c, self.j)

    def peers(self):
        found = [self.partner]
        found += [self.row_peer(d) for d in range(1, self.R)]
        found += [self.level_peer(e) for e in range(1, self.Z)]
        return found

    def greet(self):
        barrier = pltpu.get_barrier_semaphore()
        for peer in self.peers():
            pl.semaphore_signal(barrier, inc=1, device_id=peer, device_id_type=MESH)

    def meet(self):
        pl.semaphore_wait(pltpu.get_barrier_semaphore(), len(self.peers()))


class Lane:
    def __init__(self, send, recv):
        self.send, self.recv, self.open = send, recv, []

    def make(self, at, source, target, device):
        return pltpu.make_async_remote_copy(
            src_ref=source, dst_ref=target, send_sem=self.send.at[at], recv_sem=self.recv.at[at],
            device_id=device, device_id_type=MESH,
        )

    def start(self, at, source, target, device):
        copy = self.make(at, source, target, device)
        copy.start()
        self.open.append(copy)

    def arrive(self, at, target, device):
        self.make(at, target, target, device).wait_recv()

    def close(self):
        for copy in self.open:
            copy.wait_send()


def reduce_count(shards, levels):
    return 4 * shards + 2 * levels


def reduce_scratch(parts, shards, piece, width, kind):
    levels = parts // 2
    block = (levels, piece, width)
    return [
        pltpu.VMEM((2 * shards * levels, piece, width), kind),
        pltpu.VMEM((2 * shards * levels, piece, width), kind),
        pltpu.VMEM((shards,) + block, kind),
        pltpu.VMEM((shards,) + block, kind),
        pltpu.VMEM((shards,) + block, kind),
        pltpu.VMEM(block, F32),
        pltpu.VMEM(block, kind),
        pltpu.VMEM(block, kind),
        pltpu.SemaphoreType.DMA((reduce_count(shards, levels),)),
        pltpu.SemaphoreType.DMA((reduce_count(shards, levels),)),
    ]


def reduce_all(net, scratch, scale):
    src, out, pair, near, half, acc, quarter, far, send, recv = scratch
    R, Z, kind = net.R, net.Z, out.dtype
    lane = Lane(send, recv)
    a, b, e, f, c, d = 0, R, 2 * R, 3 * R, 4 * R, 4 * R + Z

    def block(core, row):
        return pl.ds((core * R + row) * Z, Z)

    order = list(range(1, R)) + [0]
    for s in order:
        lane.start(a + s, src.at[block(net.other, net.row(s))], pair.at[s], net.partner)
    for s in order:
        lane.arrive(a + s, pair.at[s], net.partner)
        total = src[block(net.c, net.row(s))].astype(F32) + pair[s].astype(F32)
        if s == 0:
            acc[...] = total
        else:
            half[s] = total.astype(kind)
            lane.start(b + s, half.at[s], near.at[s], net.row_peer(s))
    for s in range(1, R):
        lane.arrive(b + s, near.at[s], net.row_peer(-s))
        acc[...] = acc[...] + near[s].astype(F32)
    quarter[...] = acc[...].astype(kind)
    for s in range(1, Z):
        lane.start(c + s, quarter.at[net.level(s)], far.at[s], net.level_peer(s))
    total = acc[net.z]
    for s in range(1, Z):
        lane.arrive(c + s, far.at[s], net.level_peer(-s))
        total = total + far[s].astype(F32)
    base = (net.c * R + net.j) * Z
    out[base + net.z] = (total * scale).astype(kind)
    mine = out.at[base + net.z]
    for s in range(1, Z):
        lane.start(d + s, mine, mine, net.level_peer(s))
    for s in range(1, Z):
        lane.arrive(d + s, out.at[base + net.level(-s)], net.level_peer(-s))
    whole = out.at[block(net.c, net.j)]
    for s in range(1, R):
        lane.start(e + s, whole, whole, net.row_peer(s))
    lane.start(f, whole, whole, net.partner)
    for s in range(1, R):
        came = out.at[block(net.c, net.row(-s))]
        lane.arrive(e + s, came, net.row_peer(-s))
        lane.start(f + s, came, came, net.partner)
    for s in range(R):
        lane.arrive(f + s, out.at[block(net.other, net.row(-s))], net.partner)
    lane.close()


def front_kernel(parts, shards, momentum, gradient, right, kept, mean_out, gram_out,
                 mom, grad, comb, gathered, left, pair, half, far, mean, mom_sem, grad_sem, keep_sem,
                 out_sem, send, recv, *scratch):
    net = Net(parts, shards)
    P, R, Z = net.P, net.R, net.Z
    for p in range(P):
        pltpu.make_async_copy(momentum.at[p], mom.at[p], mom_sem.at[p]).start()
        pltpu.make_async_copy(gradient.at[p], grad.at[p], grad_sem.at[p]).start()
    net.greet()
    net.meet()
    lane = Lane(send, recv)
    a, b, c, d = 0, R, 2 * R, 2 * R + Z
    for s in range(1, R):
        lane.start(a + s, right.at[net.c], gathered.at[net.j, net.c], net.row_peer(s))
    gathered[net.j] = right[...]

    def combine(p, carry):
        pltpu.make_async_copy(momentum.at[p], mom.at[p], mom_sem.at[p]).wait()
        pltpu.make_async_copy(gradient.at[p], grad.at[p], grad_sem.at[p]).wait()
        comb[p] = (mom[p] + grad[p].astype(F32)).astype(BF16)
        pltpu.make_async_copy(comb.at[p], kept.at[p], keep_sem.at[p]).start()
        return carry

    lax.fori_loop(0, P, combine, 0)
    for s in range(1, R):
        came = gathered.at[net.row(-s), net.c]
        lane.arrive(a + s, came, net.row_peer(-s))
        lane.start(b + s, came, came, net.partner)
    for s in range(1, R):
        lane.arrive(b + s, gathered.at[net.row(-s), net.other], net.partner)

    def project(p):
        full = gathered[...].reshape(comb.shape[2], right.shape[2])
        left[p] = jnp.dot(comb[p], full, preferred_element_type=F32).astype(BF16)

    def hand_on(s):
        level = net.level(s)
        lane.arrive(c + s % Z, pair.at[s % Z], net.partner)
        if s < Z:
            half[s] = (left[2 * level + net.c].astype(F32) + pair[s].astype(F32)).astype(BF16)
            lane.start(d + s, half.at[s], far.at[s], net.level_peer(s))

    for s in range(1, Z + 1):
        level = net.level(s)
        project(2 * level + net.other)
        lane.start(c + s % Z, left.at[2 * level + net.other], pair.at[s % Z], net.partner)
        project(2 * level + net.c)
        if s > 1:
            hand_on(s - 1)
    hand_on(Z)
    total = left[net.r].astype(F32) + pair[0].astype(F32)
    for s in range(1, Z):
        lane.arrive(d + s, far.at[s], net.level_peer(-s))
        total = total + far[s].astype(F32)
    mean[...] = total / P
    keep_mean = pltpu.make_async_copy(mean, mean_out, out_sem.at[0])
    keep_mean.start()
    gram = dot_tn(mean[...], mean[...])
    src = scratch[0]
    pieces, piece, _ = src.shape
    for i in range(pieces):
        src[i] = gram[i * piece:(i + 1) * piece, :]
    reduce_all(net, scratch, 1.0)
    keep_gram = pltpu.make_async_copy(scratch[1], gram_out, out_sem.at[1])
    keep_gram.start()
    keep_mean.wait()
    keep_gram.wait()
    lane.close()
    for p in range(P):
        pltpu.make_async_copy(comb.at[p], kept.at[p], keep_sem.at[p]).wait()


def front(momentum, gradient, right):
    parts, shards = lax.axis_size("rep"), lax.axis_size("rows")
    levels = parts // 2
    _, rows, cols = momentum.shape
    rows = rows // parts
    depth, width = right.shape
    piece = width // (shards * parts)
    anywhere = pl.BlockSpec(memory_space=pl.ANY)
    inside = pl.BlockSpec(memory_space=pltpu.VMEM)
    count = 2 * shards + 2 * levels
    return pl.pallas_call(
        functools.partial(front_kernel, parts, shards),
        out_shape=[
            jax.ShapeDtypeStruct((parts, rows, cols), BF16),
            jax.ShapeDtypeStruct((rows, width), F32),
            jax.ShapeDtypeStruct((shards * parts, piece, width), F32),
        ],
        in_specs=[anywhere, anywhere, inside],
        out_specs=[anywhere, anywhere, anywhere],
        scratch_shapes=[
            pltpu.VMEM((parts, rows, cols), F32),
            pltpu.VMEM((parts, rows, cols), BF16),
            pltpu.VMEM((parts, rows, cols), BF16),
            pltpu.VMEM((shards, 2, depth // 2, width), BF16),
            pltpu.VMEM((parts, rows, width), BF16),
            pltpu.VMEM((levels, rows, width), BF16),
            pltpu.VMEM((levels, rows, width), BF16),
            pltpu.VMEM((levels, rows, width), BF16),
            pltpu.VMEM((rows, width), F32),
            pltpu.SemaphoreType.DMA((parts,)),
            pltpu.SemaphoreType.DMA((parts,)),
            pltpu.SemaphoreType.DMA((parts,)),
            pltpu.SemaphoreType.DMA((2,)),
            pltpu.SemaphoreType.DMA((count,)),
            pltpu.SemaphoreType.DMA((count,)),
        ] + reduce_scratch(parts, shards, piece, width, F32),
        compiler_params=pltpu.CompilerParams(collective_id=1, has_side_effects=True, vmem_limit_bytes=60 * 1024 * 1024),
        name="front",
    )(
        momentum.reshape(parts, rows, cols),
        gradient.reshape(parts, rows, cols),
        right.reshape(2, depth // 2, width),
    )


def back_kernel(parts, shards, tile, mean, inverse, kept, left_out, right_out,
                comb, left, partial, comb_sem, out_sem, send, recv, *scratch):
    net = Net(parts, shards)
    P, R, Z = net.P, net.R, net.Z
    net.greet()
    for p in range(P):
        pltpu.make_async_copy(kept.at[p], comb.at[p], comb_sem.at[p]).start()
    own = lax.dot_general(
        mean[...], inverse[...], (((1,), (1,)), ((), ())), precision=HI, preferred_element_type=F32
    )
    left[net.r] = own.astype(BF16)
    for p in range(P):
        pltpu.make_async_copy(kept.at[p], comb.at[p], comb_sem.at[p]).wait()
    net.meet()
    lane = Lane(send, recv)
    a, b = 0, Z
    mine = left.at[net.r]
    for s in range(1, Z):
        lane.start(a + s, mine, mine, net.level_peer(s))
    lane.start(b, mine, mine, net.partner)
    src = scratch[0]
    piece = src.shape[1]

    def absorb(s):
        level = net.level(-s)
        lane.arrive(b + s, left.at[2 * level + net.other], net.partner)

        def columns(t, carry):
            at = pl.ds(pl.multiple_of(t * tile, tile), tile)
            total = None
            for core in range(2):
                term = lax.dot_general(
                    comb[2 * level + core, :, at], left[2 * level + core],
                    (((0,), (0,)), ((), ())), preferred_element_type=F32,
                )
                total = term if total is None else total + term
            if s > 0:
                total = total + partial[at, :]
            if s < Z - 1:
                partial[at, :] = total
            else:
                here = pl.ds(t * (tile // piece), tile // piece)
                src[here] = total.reshape(tile // piece, piece, total.shape[1]).astype(BF16)
            return carry

        lax.fori_loop(0, partial.shape[0] // tile, columns, 0)

    for s in range(1, Z):
        came = left.at[2 * net.level(-s) + net.c]
        lane.arrive(a + s, came, net.level_peer(-s))
        lane.start(b + s, came, came, net.partner)
        absorb(s - 1)
    absorb(Z - 1)
    keep_left = pltpu.make_async_copy(left, left_out, out_sem.at[0])
    keep_left.start()
    reduce_all(net, scratch, 1.0 / P)
    keep_right = pltpu.make_async_copy(scratch[1], right_out, out_sem.at[1])
    keep_right.start()
    keep_left.wait()
    keep_right.wait()
    lane.close()


def back(mean, inverse, kept):
    parts, shards = lax.axis_size("rep"), lax.axis_size("rows")
    levels = parts // 2
    _, rows, cols = kept.shape
    width = mean.shape[1]
    piece = cols // (shards * parts)
    anywhere = pl.BlockSpec(memory_space=pl.ANY)
    inside = pl.BlockSpec(memory_space=pltpu.VMEM)
    return pl.pallas_call(
        functools.partial(back_kernel, parts, shards, 256),
        out_shape=[
            jax.ShapeDtypeStruct((parts, rows, width), BF16),
            jax.ShapeDtypeStruct((shards * parts, piece, width), BF16),
        ],
        in_specs=[inside, inside, anywhere],
        out_specs=[anywhere, anywhere],
        scratch_shapes=[
            pltpu.VMEM((parts, rows, cols), BF16),
            pltpu.VMEM((parts, rows, width), BF16),
            pltpu.VMEM((cols, width), F32),
            pltpu.SemaphoreType.DMA((parts,)),
            pltpu.SemaphoreType.DMA((2,)),
            pltpu.SemaphoreType.DMA((2 * levels,)),
            pltpu.SemaphoreType.DMA((2 * levels,)),
        ] + reduce_scratch(parts, shards, piece, width, BF16),
        compiler_params=pltpu.CompilerParams(collective_id=2, has_side_effects=True, vmem_limit_bytes=60 * 1024 * 1024),
        name="back",
    )(mean, inverse, kept)


def per_device(weights, momentum, gradient, right_factor):
    shards = lax.axis_size("rows")
    kept, mean, gram = front(momentum, gradient, right_factor.astype(BF16))
    width = right_factor.shape[1]
    inverse = inverse_factor(gram.reshape(width, width))
    left_parts, right_parts = back(mean, inverse, kept)
    left_half = left_parts.reshape(weights.shape[0], width)
    right_half = right_parts.reshape(weights.shape[1], width)
    right_mean = right_half.astype(F32)
    normed = right_mean / jnp.sqrt(jnp.mean(right_mean * right_mean, axis=0) + tiny)
    feedback = jnp.dot(left_half, right_half.T, preferred_element_type=F32)
    update = jnp.dot(left_half, normed.astype(BF16).T, preferred_element_type=F32)
    share = weights.shape[1] // shards
    new_right = lax.dynamic_slice_in_dim(normed, lax.axis_index("rows") * share, share, 0)
    new_momentum = momentum[0] + gradient[0].astype(F32) - momentum_keep * feedback
    new_weights = (weights.astype(F32) - learn_rate * jnp.sqrt(M / N) * update).astype(BF16)
    return (new_weights, new_momentum[None], new_right)


def solution(mesh):
    in_specs = (P("rows", None), P("rep", "rows", None), P("rep", "rows", None), P("rows", None))
    out_specs = (P("rows", None), P("rep", "rows", None), P("rows", None))
    return jax.shard_map(
        per_device, mesh=mesh, in_specs=in_specs, out_specs=out_specs, check_vma=False
    )
```

```python
import functools
import math

import jax, jax.numpy as jnp
from jax import lax
from jax.experimental import pallas as pl
from jax.experimental.pallas import tpu as pltpu
from jax.sharding import PartitionSpec as P

M = 7168
N = 2048


momentum_keep = 0.05
learn_rate = 0.5
tiny = 1e-06


HI = lax.Precision.HIGHEST
F32 = jnp.float32

def dot_tn(a, b):
    return lax.dot_general(a, b, (((0,), (0,)), ((), ())), precision=HI, preferred_element_type=F32)

def factor_block(work, size, step):
    wide = 2 * size
    for at in range(0, size, step):
        panel = work[at:at + step, :]
        el = {}
        for i in range(step):
            for k in range(i + 1):
                el[i, k] = jnp.broadcast_to(panel[k:k + 1, at + i:at + i + 1], (1, size))
        rows = [(panel[i:i + 1, :size], panel[i:i + 1, size:]) for i in range(step)]
        done = []
        for k in range(step):
            inv = lax.rsqrt(el[k, k])
            own = (rows[k][0] * inv, rows[k][1] * inv)
            done.append(own)
            col = {i: el[i, k] * inv for i in range(k + 1, step)}
            for i in range(k + 1, step):
                rows[i] = (rows[i][0] - col[i] * own[0], rows[i][1] - col[i] * own[1])
                for m in range(k + 1, i + 1):
                    el[i, m] = el[i, m] - col[i] * col[m]
        upper = jnp.concatenate([d[0] for d in done], axis=0)
        aug = jnp.concatenate([d[1] for d in done], axis=0)
        work[at:at + step, :size] = upper
        work[at:at + step, size:] = aug
        nxt = at + step
        if nxt < size:
            upd = dot_tn(upper, jnp.concatenate([upper, aug], axis=1))
            work[nxt:, :] = work[nxt:, :] - upd[nxt:, :]

def chol_kernel(size, step, gram_ref, out_ref, full, work):
    rank = full.shape[0]
    stacks, slots = packing(rank)
    full[:, :rank] = jnp.zeros((rank, rank), F32)
    for (i, k), (stack, at) in slots.items():
        block = gram_ref[stack * BLOCK:(stack + 1) * BLOCK, at:at + BLOCK]
        full[i * BLOCK:(i + 1) * BLOCK, k * BLOCK:(k + 1) * BLOCK] = block
    r = lax.broadcasted_iota(jnp.int32, (rank, rank), 0)
    c = lax.broadcasted_iota(jnp.int32, (rank, rank), 1)
    full[:, rank:] = jnp.where(r == c, 1.0, 0.0).astype(F32)
    rb = lax.broadcasted_iota(jnp.int32, (size, size), 0)
    cb = lax.broadcasted_iota(jnp.int32, (size, size), 1)
    eye = jnp.where(rb == cb, 1.0, 0.0).astype(F32)
    for at in range(0, rank, size):
        work[:, :size] = full[at:at + size, at:at + size]
        work[:, size:] = eye
        factor_block(work, size, step)
        inv = jnp.where(rb >= cb, work[:, size:], 0.0)
        block = jnp.dot(inv, full[at:at + size, :], precision=HI, preferred_element_type=F32)
        out_ref[at:at + size, :] = block[:, rank:]
        nxt = at + size
        if nxt < rank:
            full[nxt:, :] = full[nxt:, :] - dot_tn(block[:, nxt:rank], block)

def inverse_factor(gram, rank):
    size = BLOCK
    return pl.pallas_call(
        lambda *refs: chol_kernel(size, 16, *refs),
        out_shape=jax.ShapeDtypeStruct((rank, rank), F32),
        in_specs=[pl.BlockSpec(memory_space=pltpu.VMEM)],
        out_specs=pl.BlockSpec(memory_space=pltpu.VMEM),
        scratch_shapes=[pltpu.VMEM((rank, 2 * rank), F32), pltpu.VMEM((size, 2 * size), F32)],
        name="inverse_factor",
    )(gram)


MESH = pl.DeviceIdType.MESH
BF16 = jnp.bfloat16


class Net:
    def __init__(self, parts, shards):
        self.P, self.R, self.Z = parts, shards, parts // 2
        self.r, self.j = lax.axis_index("rep"), lax.axis_index("rows")
        self.z, self.c = self.r // 2, lax.rem(self.r, 2)
        self.other = 1 - self.c
        self.partner = (2 * self.z + self.other, self.j)

    def row(self, step):
        return lax.rem(self.j + step + self.R, self.R)

    def level(self, step):
        return lax.rem(self.z + step + self.Z, self.Z)

    def row_peer(self, step):
        return (self.r, self.row(step))

    def level_peer(self, step):
        return (2 * self.level(step) + self.c, self.j)

    def peers(self):
        found = [self.partner]
        found += [self.row_peer(d) for d in range(1, self.R)]
        found += [self.level_peer(e) for e in range(1, self.Z)]
        return found

    def greet(self):
        barrier = pltpu.get_barrier_semaphore()
        for peer in self.peers():
            pl.semaphore_signal(barrier, inc=1, device_id=peer, device_id_type=MESH)

    def meet(self):
        pl.semaphore_wait(pltpu.get_barrier_semaphore(), len(self.peers()))


class Lane:
    def __init__(self, send, recv):
        self.send, self.recv, self.open = send, recv, []

    def make(self, at, source, target, device):
        return pltpu.make_async_remote_copy(
            src_ref=source, dst_ref=target, send_sem=self.send.at[at], recv_sem=self.recv.at[at],
            device_id=device, device_id_type=MESH,
        )

    def start(self, at, source, target, device):
        copy = self.make(at, source, target, device)
        copy.start()
        self.open.append(copy)

    def arrive(self, at, target, device):
        self.make(at, target, target, device).wait_recv()

    def close(self):
        for copy in self.open:
            copy.wait_send()


def reduce_count(shards, levels):
    return 4 * shards + 2 * levels


def reduce_scratch(parts, shards, piece, width, kind):
    levels = parts // 2
    block = (levels, piece, width)
    return [
        pltpu.VMEM((2 * shards * levels, piece, width), kind),
        pltpu.VMEM((2 * shards * levels, piece, width), kind),
        pltpu.VMEM((shards,) + block, kind),
        pltpu.VMEM((shards,) + block, kind),
        pltpu.VMEM((shards,) + block, kind),
        pltpu.VMEM(block, F32),
        pltpu.VMEM(block, kind),
        pltpu.VMEM(block, kind),
        pltpu.SemaphoreType.DMA((reduce_count(shards, levels),)),
        pltpu.SemaphoreType.DMA((reduce_count(shards, levels),)),
    ]


def reduce_all(net, scratch, scale):
    src, out, pair, near, half, acc, quarter, far, send, recv = scratch
    R, Z, kind = net.R, net.Z, out.dtype
    lane = Lane(send, recv)
    a, b, e, f, c, d = 0, R, 2 * R, 3 * R, 4 * R, 4 * R + Z

    def block(core, row):
        return pl.ds((core * R + row) * Z, Z)

    order = list(range(1, R)) + [0]
    for s in order:
        lane.start(a + s, src.at[block(net.other, net.row(s))], pair.at[s], net.partner)
    for s in order:
        lane.arrive(a + s, pair.at[s], net.partner)
        total = src[block(net.c, net.row(s))].astype(F32) + pair[s].astype(F32)
        if s == 0:
            acc[...] = total
        else:
            half[s] = total.astype(kind)
            lane.start(b + s, half.at[s], near.at[s], net.row_peer(s))
    for s in range(1, R):
        lane.arrive(b + s, near.at[s], net.row_peer(-s))
        acc[...] = acc[...] + near[s].astype(F32)
    quarter[...] = acc[...].astype(kind)
    for s in range(1, Z):
        lane.start(c + s, quarter.at[net.level(s)], far.at[s], net.level_peer(s))
    total = acc[net.z]
    for s in range(1, Z):
        lane.arrive(c + s, far.at[s], net.level_peer(-s))
        total = total + far[s].astype(F32)
    base = (net.c * R + net.j) * Z
    out[base + net.z] = (total * scale).astype(kind)
    mine = out.at[base + net.z]
    for s in range(1, Z):
        lane.start(d + s, mine, mine, net.level_peer(s))
    for s in range(1, Z):
        lane.arrive(d + s, out.at[base + net.level(-s)], net.level_peer(-s))
    whole = out.at[block(net.c, net.j)]
    for s in range(1, R):
        lane.start(e + s, whole, whole, net.row_peer(s))
    lane.start(f, whole, whole, net.partner)
    for s in range(1, R):
        came = out.at[block(net.c, net.row(-s))]
        lane.arrive(e + s, came, net.row_peer(-s))
        lane.start(f + s, came, came, net.partner)
    for s in range(R):
        lane.arrive(f + s, out.at[block(net.other, net.row(-s))], net.partner)
    lane.close()


BLOCK = 128


def packing(width):
    count = width // BLOCK
    names = [(i, k) for i in range(count) for k in range(i, count)]
    stacks = 2 if len(names) % 2 == 0 else 1
    each = len(names) // stacks
    return stacks, {name: (n // each, (n % each) * BLOCK) for n, name in enumerate(names)}


def packed_shape(width, pieces):
    stacks, slots = packing(width)
    return pieces, stacks * BLOCK // pieces, len(slots) // stacks * BLOCK


def front_kernel(parts, shards, momentum, gradient, right, kept, mean_out, gram_out,
                 mom, grad, comb, gathered, left, pair, half, far, mean, mom_sem, grad_sem, keep_sem,
                 out_sem, send, recv, *scratch):
    net = Net(parts, shards)
    P, R, Z = net.P, net.R, net.Z
    for p in range(P):
        pltpu.make_async_copy(momentum.at[p], mom.at[p], mom_sem.at[p]).start()
        pltpu.make_async_copy(gradient.at[p], grad.at[p], grad_sem.at[p]).start()
    net.greet()
    net.meet()
    lane = Lane(send, recv)
    a, b, c, d = 0, R, 2 * R, 2 * R + Z
    for s in range(1, R):
        lane.start(a + s, right.at[net.c], gathered.at[net.j, net.c], net.row_peer(s))
    gathered[net.j] = right[...]

    def combine(p, carry):
        pltpu.make_async_copy(momentum.at[p], mom.at[p], mom_sem.at[p]).wait()
        pltpu.make_async_copy(gradient.at[p], grad.at[p], grad_sem.at[p]).wait()
        comb[p] = (mom[p] + grad[p].astype(F32)).astype(BF16)
        pltpu.make_async_copy(comb.at[p], kept.at[p], keep_sem.at[p]).start()
        return carry

    lax.fori_loop(0, P, combine, 0)
    for s in range(1, R):
        came = gathered.at[net.row(-s), net.c]
        lane.arrive(a + s, came, net.row_peer(-s))
        lane.start(b + s, came, came, net.partner)
    for s in range(1, R):
        lane.arrive(b + s, gathered.at[net.row(-s), net.other], net.partner)

    def project(p):
        full = gathered[...].reshape(comb.shape[2], right.shape[2])
        left[p] = jnp.dot(comb[p], full, preferred_element_type=F32).astype(BF16)

    def hand_on(s):
        level = net.level(s)
        lane.arrive(c + s % Z, pair.at[s % Z], net.partner)
        if s < Z:
            half[s] = (left[2 * level + net.c].astype(F32) + pair[s].astype(F32)).astype(BF16)
            lane.start(d + s, half.at[s], far.at[s], net.level_peer(s))

    for s in range(1, Z + 1):
        level = net.level(s)
        project(2 * level + net.other)
        lane.start(c + s % Z, left.at[2 * level + net.other], pair.at[s % Z], net.partner)
        project(2 * level + net.c)
        if s > 1:
            hand_on(s - 1)
    hand_on(Z)
    total = left[net.r].astype(F32) + pair[0].astype(F32)
    for s in range(1, Z):
        lane.arrive(d + s, far.at[s], net.level_peer(-s))
        total = total + far[s].astype(F32)
    mean[...] = total / P
    keep_mean = pltpu.make_async_copy(mean, mean_out, out_sem.at[0])
    keep_mean.start()
    src = scratch[0]
    pieces, piece, _ = src.shape
    stacks, slots = packing(mean.shape[1])
    spread = BLOCK // (pieces // stacks)
    for i in range(mean.shape[1] // BLOCK):
        gram = dot_tn(mean[:, i * BLOCK:(i + 1) * BLOCK], mean[:, i * BLOCK:])
        for k in range(i, mean.shape[1] // BLOCK):
            stack, at = slots[i, k]
            block = gram[:, (k - i) * BLOCK:(k - i + 1) * BLOCK]
            for m in range(pieces // stacks):
                src[stack * (pieces // stacks) + m, :, at:at + BLOCK] = block[m * spread:(m + 1) * spread, :]
    reduce_all(net, scratch, 1.0)
    keep_gram = pltpu.make_async_copy(scratch[1], gram_out, out_sem.at[1])
    keep_gram.start()
    keep_mean.wait()
    keep_gram.wait()
    lane.close()
    for p in range(P):
        pltpu.make_async_copy(comb.at[p], kept.at[p], keep_sem.at[p]).wait()


def front(momentum, gradient, right):
    parts, shards = lax.axis_size("rep"), lax.axis_size("rows")
    levels = parts // 2
    _, rows, cols = momentum.shape
    rows = rows // parts
    depth, width = right.shape
    packed = packed_shape(width, shards * parts)
    anywhere = pl.BlockSpec(memory_space=pl.ANY)
    inside = pl.BlockSpec(memory_space=pltpu.VMEM)
    count = 2 * shards + 2 * levels
    return pl.pallas_call(
        functools.partial(front_kernel, parts, shards),
        out_shape=[
            jax.ShapeDtypeStruct((parts, rows, cols), BF16),
            jax.ShapeDtypeStruct((rows, width), F32),
            jax.ShapeDtypeStruct(packed, F32),
        ],
        in_specs=[anywhere, anywhere, inside],
        out_specs=[anywhere, anywhere, anywhere],
        scratch_shapes=[
            pltpu.VMEM((parts, rows, cols), F32),
            pltpu.VMEM((parts, rows, cols), BF16),
            pltpu.VMEM((parts, rows, cols), BF16),
            pltpu.VMEM((shards, 2, depth // 2, width), BF16),
            pltpu.VMEM((parts, rows, width), BF16),
            pltpu.VMEM((levels, rows, width), BF16),
            pltpu.VMEM((levels, rows, width), BF16),
            pltpu.VMEM((levels, rows, width), BF16),
            pltpu.VMEM((rows, width), F32),
            pltpu.SemaphoreType.DMA((parts,)),
            pltpu.SemaphoreType.DMA((parts,)),
            pltpu.SemaphoreType.DMA((parts,)),
            pltpu.SemaphoreType.DMA((2,)),
            pltpu.SemaphoreType.DMA((count,)),
            pltpu.SemaphoreType.DMA((count,)),
        ] + reduce_scratch(parts, shards, packed[1], packed[2], F32),
        compiler_params=pltpu.CompilerParams(collective_id=1, has_side_effects=True, vmem_limit_bytes=60 * 1024 * 1024),
        name="front",
    )(
        momentum.reshape(parts, rows, cols),
        gradient.reshape(parts, rows, cols),
        right.reshape(2, depth // 2, width),
    )


def back_kernel(parts, shards, tile, mean, inverse, kept, left_out, right_out,
                comb, left, partial, comb_sem, out_sem, send, recv, *scratch):
    net = Net(parts, shards)
    P, R, Z = net.P, net.R, net.Z
    net.greet()
    for p in range(P):
        pltpu.make_async_copy(kept.at[p], comb.at[p], comb_sem.at[p]).start()
    own = lax.dot_general(
        mean[...], inverse[...], (((1,), (1,)), ((), ())), precision=HI, preferred_element_type=F32
    )
    left[net.r] = own.astype(BF16)
    for p in range(P):
        pltpu.make_async_copy(kept.at[p], comb.at[p], comb_sem.at[p]).wait()
    net.meet()
    lane = Lane(send, recv)
    a, b = 0, Z
    mine = left.at[net.r]
    for s in range(1, Z):
        lane.start(a + s, mine, mine, net.level_peer(s))
    lane.start(b, mine, mine, net.partner)
    src = scratch[0]
    piece = src.shape[1]

    def absorb(s):
        level = net.level(-s)
        lane.arrive(b + s, left.at[2 * level + net.other], net.partner)

        def columns(t, carry):
            at = pl.ds(pl.multiple_of(t * tile, tile), tile)
            total = None
            for core in range(2):
                term = lax.dot_general(
                    comb[2 * level + core, :, at], left[2 * level + core],
                    (((0,), (0,)), ((), ())), preferred_element_type=F32,
                )
                total = term if total is None else total + term
            if s > 0:
                total = total + partial[at, :]
            if s < Z - 1:
                partial[at, :] = total
            else:
                here = pl.ds(t * (tile // piece), tile // piece)
                src[here] = total.reshape(tile // piece, piece, total.shape[1]).astype(BF16)
            return carry

        lax.fori_loop(0, partial.shape[0] // tile, columns, 0)

    for s in range(1, Z):
        came = left.at[2 * net.level(-s) + net.c]
        lane.arrive(a + s, came, net.level_peer(-s))
        lane.start(b + s, came, came, net.partner)
        absorb(s - 1)
    absorb(Z - 1)
    keep_left = pltpu.make_async_copy(left, left_out, out_sem.at[0])
    keep_left.start()
    reduce_all(net, scratch, 1.0 / P)
    keep_right = pltpu.make_async_copy(scratch[1], right_out, out_sem.at[1])
    keep_right.start()
    keep_left.wait()
    keep_right.wait()
    lane.close()


def back(mean, inverse, kept):
    parts, shards = lax.axis_size("rep"), lax.axis_size("rows")
    levels = parts // 2
    _, rows, cols = kept.shape
    width = mean.shape[1]
    piece = cols // (shards * parts)
    anywhere = pl.BlockSpec(memory_space=pl.ANY)
    inside = pl.BlockSpec(memory_space=pltpu.VMEM)
    return pl.pallas_call(
        functools.partial(back_kernel, parts, shards, 256),
        out_shape=[
            jax.ShapeDtypeStruct((parts, rows, width), BF16),
            jax.ShapeDtypeStruct((shards * parts, piece, width), BF16),
        ],
        in_specs=[inside, inside, anywhere],
        out_specs=[anywhere, anywhere],
        scratch_shapes=[
            pltpu.VMEM((parts, rows, cols), BF16),
            pltpu.VMEM((parts, rows, width), BF16),
            pltpu.VMEM((cols, width), F32),
            pltpu.SemaphoreType.DMA((parts,)),
            pltpu.SemaphoreType.DMA((2,)),
            pltpu.SemaphoreType.DMA((2 * levels,)),
            pltpu.SemaphoreType.DMA((2 * levels,)),
        ] + reduce_scratch(parts, shards, piece, width, BF16),
        compiler_params=pltpu.CompilerParams(collective_id=2, has_side_effects=True, vmem_limit_bytes=60 * 1024 * 1024),
        name="back",
    )(mean, inverse, kept)


def final_kernel(scale, left, right, weights, momentum, gradient, weights_out, momentum_out, right_out, normed):
    share = right_out.shape[0]

    @pl.when(pl.program_id(0) == 0)
    def _():
        mean = right[...].astype(F32)
        length = jnp.sqrt(jnp.mean(mean * mean, axis=0, keepdims=True) + tiny)
        normed[...] = (mean / length).astype(BF16)
        at = pl.ds(pl.multiple_of(lax.axis_index("rows") * share, share), share)
        right_out[...] = right[at, :].astype(F32) / length

    nt = (((1,), (1,)), ((), ()))
    feedback = lax.dot_general(left[...], right[...], nt, preferred_element_type=F32)
    momentum_out[...] = momentum[...] + gradient[...].astype(F32) - momentum_keep * feedback
    update = lax.dot_general(left[...], normed[...], nt, preferred_element_type=F32)
    weights_out[...] = (weights[...].astype(F32) - scale * update).astype(BF16)


def final(left, right, weights, momentum, gradient):
    rows, cols = weights.shape
    width = right.shape[1]
    share = cols // lax.axis_size("rows")
    tile = next(t for t in (256, 224, 128, 64, 32, 16, 8) if rows % t == 0)
    scale = learn_rate * math.sqrt(M / N)

    def streamed(columns):
        return pl.BlockSpec((tile, columns), lambda i: (i, 0))

    def fixed(shape):
        return pl.BlockSpec(shape, lambda i: (0, 0))

    return pl.pallas_call(
        functools.partial(final_kernel, scale),
        grid=(rows // tile,),
        out_shape=[
            jax.ShapeDtypeStruct((rows, cols), BF16),
            jax.ShapeDtypeStruct((rows, cols), F32),
            jax.ShapeDtypeStruct((share, width), F32),
        ],
        in_specs=[streamed(width), fixed((cols, width)), streamed(cols), streamed(cols), streamed(cols)],
        out_specs=[streamed(cols), streamed(cols), fixed((share, width))],
        scratch_shapes=[pltpu.VMEM((cols, width), BF16)],
        compiler_params=pltpu.CompilerParams(vmem_limit_bytes=60 * 1024 * 1024),
        name="final",
    )(left, right, weights, momentum, gradient)


def per_device(weights, momentum, gradient, right_factor):
    kept, mean, gram = front(momentum, gradient, right_factor.astype(BF16))
    width = right_factor.shape[1]
    inverse = inverse_factor(gram.reshape(-1, gram.shape[2]), width)
    left_parts, right_parts = back(mean, inverse, kept)
    left_half = left_parts.reshape(weights.shape[0], width)
    right_half = right_parts.reshape(weights.shape[1], width)
    new_weights, new_momentum, new_right = final(left_half, right_half, weights, momentum[0], gradient[0])
    return (new_weights, new_momentum[None], new_right)


def solution(mesh):
    in_specs = (P("rows", None), P("rep", "rows", None), P("rep", "rows", None), P("rows", None))
    out_specs = (P("rows", None), P("rep", "rows", None), P("rows", None))
    return jax.shard_map(
        per_device, mesh=mesh, in_specs=in_specs, out_specs=out_specs, check_vma=False
    )
```

```python
import functools
import math

import jax, jax.numpy as jnp
from jax import lax
from jax.experimental import pallas as pl
from jax.experimental.pallas import tpu as pltpu
from jax.sharding import PartitionSpec as P

M = 7168
N = 2048


momentum_keep = 0.05
learn_rate = 0.5
tiny = 1e-06


HI = lax.Precision.HIGHEST
F32 = jnp.float32

def dot_tn(a, b):
    return lax.dot_general(a, b, (((0,), (0,)), ((), ())), precision=HI, preferred_element_type=F32)

def thirds(a):
    high = a.astype(jnp.bfloat16)
    rest = a - high.astype(F32)
    middle = rest.astype(jnp.bfloat16)
    return high, middle, (rest - middle.astype(F32)).astype(jnp.bfloat16)


def dot_thin(a, b):
    ah, am, al = thirds(a)
    bh, bm, bl = thirds(b)
    lhs = jnp.concatenate([ah, ah, am, am, ah, al], axis=0)
    rhs = jnp.concatenate([bh, bm, bh, bm, bl, bh], axis=0)
    return lax.dot_general(lhs, rhs, (((0,), (0,)), ((), ())), preferred_element_type=F32)


def factor_block(work, size, step):
    wide = 2 * size
    for at in range(0, size, step):
        panel = work[at:at + step, :]
        el = {}
        for i in range(step):
            for k in range(i + 1):
                el[i, k] = jnp.broadcast_to(panel[k:k + 1, at + i:at + i + 1], (1, size))
        rows = [(panel[i:i + 1, :size], panel[i:i + 1, size:]) for i in range(step)]
        done = []
        for k in range(step):
            inv = lax.rsqrt(el[k, k])
            own = (rows[k][0] * inv, rows[k][1] * inv)
            done.append(own)
            col = {i: el[i, k] * inv for i in range(k + 1, step)}
            for i in range(k + 1, step):
                rows[i] = (rows[i][0] - col[i] * own[0], rows[i][1] - col[i] * own[1])
                for m in range(k + 1, i + 1):
                    el[i, m] = el[i, m] - col[i] * col[m]
        upper = jnp.concatenate([d[0] for d in done], axis=0)
        aug = jnp.concatenate([d[1] for d in done], axis=0)
        work[at:at + step, :size] = upper
        work[at:at + step, size:] = aug
        nxt = at + step
        if nxt < size:
            upd = dot_thin(upper, jnp.concatenate([upper, aug], axis=1))
            work[nxt:, :] = work[nxt:, :] - upd[nxt:, :]

def chol_kernel(size, step, gram_ref, out_ref, full, work):
    rank = full.shape[0]
    stacks, slots = packing(rank)
    full[:, :rank] = jnp.zeros((rank, rank), F32)
    for (i, k), (stack, at) in slots.items():
        block = gram_ref[stack * BLOCK:(stack + 1) * BLOCK, at:at + BLOCK]
        full[i * BLOCK:(i + 1) * BLOCK, k * BLOCK:(k + 1) * BLOCK] = block
    r = lax.broadcasted_iota(jnp.int32, (rank, rank), 0)
    c = lax.broadcasted_iota(jnp.int32, (rank, rank), 1)
    full[:, rank:] = jnp.where(r == c, 1.0, 0.0).astype(F32)
    rb = lax.broadcasted_iota(jnp.int32, (size, size), 0)
    cb = lax.broadcasted_iota(jnp.int32, (size, size), 1)
    eye = jnp.where(rb == cb, 1.0, 0.0).astype(F32)
    for at in range(0, rank, size):
        work[:, :size] = full[at:at + size, at:at + size]
        work[:, size:] = eye
        factor_block(work, size, step)
        inv = jnp.where(rb >= cb, work[:, size:], 0.0)
        block = jnp.dot(inv, full[at:at + size, :], precision=HI, preferred_element_type=F32)
        out_ref[at:at + size, :] = block[:, rank:]
        nxt = at + size
        if nxt < rank:
            full[nxt:, :] = full[nxt:, :] - dot_tn(block[:, nxt:rank], block)

def inverse_factor(gram, rank):
    size = BLOCK
    return pl.pallas_call(
        lambda *refs: chol_kernel(size, 16, *refs),
        out_shape=jax.ShapeDtypeStruct((rank, rank), F32),
        in_specs=[pl.BlockSpec(memory_space=pltpu.VMEM)],
        out_specs=pl.BlockSpec(memory_space=pltpu.VMEM),
        scratch_shapes=[pltpu.VMEM((rank, 2 * rank), F32), pltpu.VMEM((size, 2 * size), F32)],
        name="inverse_factor",
    )(gram)


MESH = pl.DeviceIdType.MESH
BF16 = jnp.bfloat16


class Net:
    def __init__(self, parts, shards):
        self.P, self.R, self.Z = parts, shards, parts // 2
        self.r, self.j = lax.axis_index("rep"), lax.axis_index("rows")
        self.z, self.c = self.r // 2, lax.rem(self.r, 2)
        self.other = 1 - self.c
        self.partner = (2 * self.z + self.other, self.j)

    def row(self, step):
        return lax.rem(self.j + step + self.R, self.R)

    def level(self, step):
        return lax.rem(self.z + step + self.Z, self.Z)

    def row_peer(self, step):
        return (self.r, self.row(step))

    def level_peer(self, step):
        return (2 * self.level(step) + self.c, self.j)

    def peers(self):
        found = [self.partner]
        found += [self.row_peer(d) for d in range(1, self.R)]
        found += [self.level_peer(e) for e in range(1, self.Z)]
        return found

    def greet(self):
        barrier = pltpu.get_barrier_semaphore()
        for peer in self.peers():
            pl.semaphore_signal(barrier, inc=1, device_id=peer, device_id_type=MESH)

    def meet(self):
        pl.semaphore_wait(pltpu.get_barrier_semaphore(), len(self.peers()))


class Lane:
    def __init__(self, send, recv):
        self.send, self.recv, self.open = send, recv, []

    def make(self, at, source, target, device):
        return pltpu.make_async_remote_copy(
            src_ref=source, dst_ref=target, send_sem=self.send.at[at], recv_sem=self.recv.at[at],
            device_id=device, device_id_type=MESH,
        )

    def start(self, at, source, target, device):
        copy = self.make(at, source, target, device)
        copy.start()
        self.open.append(copy)

    def arrive(self, at, target, device):
        self.make(at, target, target, device).wait_recv()

    def close(self):
        for copy in self.open:
            copy.wait_send()


def reduce_count(shards, levels):
    return 4 * shards + 2 * levels


def reduce_scratch(parts, shards, piece, width, kind):
    levels = parts // 2
    block = (levels, piece, width)
    return [
        pltpu.VMEM((2 * shards * levels, piece, width), kind),
        pltpu.VMEM((2 * shards * levels, piece, width), kind),
        pltpu.VMEM((shards,) + block, kind),
        pltpu.VMEM((shards,) + block, kind),
        pltpu.VMEM((shards,) + block, kind),
        pltpu.VMEM(block, F32),
        pltpu.VMEM(block, kind),
        pltpu.VMEM(block, kind),
        pltpu.SemaphoreType.DMA((reduce_count(shards, levels),)),
        pltpu.SemaphoreType.DMA((reduce_count(shards, levels),)),
    ]


def reduce_all(net, scratch, scale):
    src, out, pair, near, half, acc, quarter, far, send, recv = scratch
    R, Z, kind = net.R, net.Z, out.dtype
    lane = Lane(send, recv)
    a, b, e, f, c, d = 0, R, 2 * R, 3 * R, 4 * R, 4 * R + Z

    def block(core, row):
        return pl.ds((core * R + row) * Z, Z)

    order = list(range(1, R)) + [0]
    for s in order:
        lane.start(a + s, src.at[block(net.other, net.row(s))], pair.at[s], net.partner)
    for s in order:
        lane.arrive(a + s, pair.at[s], net.partner)
        total = src[block(net.c, net.row(s))].astype(F32) + pair[s].astype(F32)
        if s == 0:
            acc[...] = total
        else:
            half[s] = total.astype(kind)
            lane.start(b + s, half.at[s], near.at[s], net.row_peer(s))
    for s in range(1, R):
        lane.arrive(b + s, near.at[s], net.row_peer(-s))
        acc[...] = acc[...] + near[s].astype(F32)
    quarter[...] = acc[...].astype(kind)
    for s in range(1, Z):
        lane.start(c + s, quarter.at[net.level(s)], far.at[s], net.level_peer(s))
    total = acc[net.z]
    for s in range(1, Z):
        lane.arrive(c + s, far.at[s], net.level_peer(-s))
        total = total + far[s].astype(F32)
    base = (net.c * R + net.j) * Z
    out[base + net.z] = (total * scale).astype(kind)
    mine = out.at[base + net.z]
    for s in range(1, Z):
        lane.start(d + s, mine, mine, net.level_peer(s))
    for s in range(1, Z):
        lane.arrive(d + s, out.at[base + net.level(-s)], net.level_peer(-s))
    whole = out.at[block(net.c, net.j)]
    for s in range(1, R):
        lane.start(e + s, whole, whole, net.row_peer(s))
    lane.start(f, whole, whole, net.partner)
    for s in range(1, R):
        came = out.at[block(net.c, net.row(-s))]
        lane.arrive(e + s, came, net.row_peer(-s))
        lane.start(f + s, came, came, net.partner)
    for s in range(R):
        lane.arrive(f + s, out.at[block(net.other, net.row(-s))], net.partner)
    lane.close()


BLOCK = 128


def packing(width):
    count = width // BLOCK
    names = [(i, k) for i in range(count) for k in range(i, count)]
    stacks = 2 if len(names) % 2 == 0 else 1
    each = len(names) // stacks
    return stacks, {name: (n // each, (n % each) * BLOCK) for n, name in enumerate(names)}


def packed_shape(width, pieces):
    stacks, slots = packing(width)
    return pieces, stacks * BLOCK // pieces, len(slots) // stacks * BLOCK


def front_kernel(parts, shards, momentum, gradient, right, kept, mean_out, gram_out,
                 mom, grad, comb, gathered, left, pair, half, far, mean, mom_sem, grad_sem, keep_sem,
                 out_sem, send, recv, *scratch):
    net = Net(parts, shards)
    P, R, Z = net.P, net.R, net.Z
    for p in range(P):
        pltpu.make_async_copy(momentum.at[p], mom.at[p], mom_sem.at[p]).start()
        pltpu.make_async_copy(gradient.at[p], grad.at[p], grad_sem.at[p]).start()
    net.greet()
    gathered[net.j] = right[...].astype(BF16)
    net.meet()
    lane = Lane(send, recv)
    a, b, c, d = 0, R, 2 * R, 2 * R + Z
    for s in range(1, R):
        own = gathered.at[net.j, net.c]
        lane.start(a + s, own, own, net.row_peer(s))

    def combine(p, carry):
        pltpu.make_async_copy(momentum.at[p], mom.at[p], mom_sem.at[p]).wait()
        pltpu.make_async_copy(gradient.at[p], grad.at[p], grad_sem.at[p]).wait()
        comb[p] = (mom[p] + grad[p].astype(F32)).astype(BF16)
        pltpu.make_async_copy(comb.at[p], kept.at[p], keep_sem.at[p]).start()
        return carry

    lax.fori_loop(0, P, combine, 0)
    for s in range(1, R):
        came = gathered.at[net.row(-s), net.c]
        lane.arrive(a + s, came, net.row_peer(-s))
        lane.start(b + s, came, came, net.partner)
    for s in range(1, R):
        lane.arrive(b + s, gathered.at[net.row(-s), net.other], net.partner)

    def project(p):
        full = gathered[...].reshape(comb.shape[2], right.shape[2])
        left[p] = jnp.dot(comb[p], full, preferred_element_type=F32).astype(BF16)

    def hand_on(s):
        level = net.level(s)
        lane.arrive(c + s % Z, pair.at[s % Z], net.partner)
        if s < Z:
            half[s] = (left[2 * level + net.c].astype(F32) + pair[s].astype(F32)).astype(BF16)
            lane.start(d + s, half.at[s], far.at[s], net.level_peer(s))

    for s in range(1, Z + 1):
        level = net.level(s)
        project(2 * level + net.other)
        lane.start(c + s % Z, left.at[2 * level + net.other], pair.at[s % Z], net.partner)
        project(2 * level + net.c)
        if s > 1:
            hand_on(s - 1)
    hand_on(Z)
    total = left[net.r].astype(F32) + pair[0].astype(F32)
    for s in range(1, Z):
        lane.arrive(d + s, far.at[s], net.level_peer(-s))
        total = total + far[s].astype(F32)
    mean[...] = total / P
    keep_mean = pltpu.make_async_copy(mean, mean_out, out_sem.at[0])
    keep_mean.start()
    src = scratch[0]
    pieces, piece, _ = src.shape
    stacks, slots = packing(mean.shape[1])
    spread = BLOCK // (pieces // stacks)
    for i in range(mean.shape[1] // BLOCK):
        gram = dot_tn(mean[:, i * BLOCK:(i + 1) * BLOCK], mean[:, i * BLOCK:])
        for k in range(i, mean.shape[1] // BLOCK):
            stack, at = slots[i, k]
            block = gram[:, (k - i) * BLOCK:(k - i + 1) * BLOCK]
            for m in range(pieces // stacks):
                src[stack * (pieces // stacks) + m, :, at:at + BLOCK] = block[m * spread:(m + 1) * spread, :]
    reduce_all(net, scratch, 1.0)
    keep_gram = pltpu.make_async_copy(scratch[1], gram_out, out_sem.at[1])
    keep_gram.start()
    keep_mean.wait()
    keep_gram.wait()
    lane.close()
    for p in range(P):
        pltpu.make_async_copy(comb.at[p], kept.at[p], keep_sem.at[p]).wait()


def front(momentum, gradient, right):
    parts, shards = lax.axis_size("rep"), lax.axis_size("rows")
    levels = parts // 2
    _, rows, cols = momentum.shape
    rows = rows // parts
    depth, width = right.shape
    packed = packed_shape(width, shards * parts)
    anywhere = pl.BlockSpec(memory_space=pl.ANY)
    inside = pl.BlockSpec(memory_space=pltpu.VMEM)
    count = 2 * shards + 2 * levels
    return pl.pallas_call(
        functools.partial(front_kernel, parts, shards),
        out_shape=[
            jax.ShapeDtypeStruct((parts, rows, cols), BF16),
            jax.ShapeDtypeStruct((rows, width), F32),
            jax.ShapeDtypeStruct(packed, F32),
        ],
        in_specs=[anywhere, anywhere, inside],
        out_specs=[anywhere, anywhere, anywhere],
        scratch_shapes=[
            pltpu.VMEM((parts, rows, cols), F32),
            pltpu.VMEM((parts, rows, cols), BF16),
            pltpu.VMEM((parts, rows, cols), BF16),
            pltpu.VMEM((shards, 2, depth // 2, width), BF16),
            pltpu.VMEM((parts, rows, width), BF16),
            pltpu.VMEM((levels, rows, width), BF16),
            pltpu.VMEM((levels, rows, width), BF16),
            pltpu.VMEM((levels, rows, width), BF16),
            pltpu.VMEM((rows, width), F32),
            pltpu.SemaphoreType.DMA((parts,)),
            pltpu.SemaphoreType.DMA((parts,)),
            pltpu.SemaphoreType.DMA((parts,)),
            pltpu.SemaphoreType.DMA((2,)),
            pltpu.SemaphoreType.DMA((count,)),
            pltpu.SemaphoreType.DMA((count,)),
        ] + reduce_scratch(parts, shards, packed[1], packed[2], F32),
        compiler_params=pltpu.CompilerParams(collective_id=1, has_side_effects=True, vmem_limit_bytes=60 * 1024 * 1024),
        name="front",
    )(
        momentum.reshape(parts, rows, cols),
        gradient.reshape(parts, rows, cols),
        right.reshape(2, depth // 2, width),
    )


def back_kernel(parts, shards, tile, mean, inverse, kept, left_out, right_out,
                comb, left, partial, comb_sem, out_sem, send, recv, *scratch):
    net = Net(parts, shards)
    P, R, Z = net.P, net.R, net.Z
    net.greet()
    for p in range(P):
        pltpu.make_async_copy(kept.at[p], comb.at[p], comb_sem.at[p]).start()
    own = lax.dot_general(
        mean[...], inverse[...], (((1,), (1,)), ((), ())), precision=HI, preferred_element_type=F32
    )
    left[net.r] = own.astype(BF16)
    net.meet()
    lane = Lane(send, recv)
    a, b = 0, Z
    mine = left.at[net.r]
    for s in range(1, Z):
        lane.start(a + s, mine, mine, net.level_peer(s))
    lane.start(b, mine, mine, net.partner)
    for p in range(P):
        pltpu.make_async_copy(kept.at[p], comb.at[p], comb_sem.at[p]).wait()
    src = scratch[0]
    piece = src.shape[1]

    def absorb(s):
        level = net.level(-s)
        lane.arrive(b + s, left.at[2 * level + net.other], net.partner)

        def columns(t, carry):
            at = pl.ds(pl.multiple_of(t * tile, tile), tile)
            total = None
            for core in range(2):
                term = lax.dot_general(
                    comb[2 * level + core, :, at], left[2 * level + core],
                    (((0,), (0,)), ((), ())), preferred_element_type=F32,
                )
                total = term if total is None else total + term
            if s > 0:
                total = total + partial[at, :]
            if s < Z - 1:
                partial[at, :] = total
            else:
                here = pl.ds(t * (tile // piece), tile // piece)
                src[here] = total.reshape(tile // piece, piece, total.shape[1]).astype(BF16)
            return carry

        lax.fori_loop(0, partial.shape[0] // tile, columns, 0)

    for s in range(1, Z):
        came = left.at[2 * net.level(-s) + net.c]
        lane.arrive(a + s, came, net.level_peer(-s))
        lane.start(b + s, came, came, net.partner)
        absorb(s - 1)
    absorb(Z - 1)
    keep_left = pltpu.make_async_copy(left, left_out, out_sem.at[0])
    keep_left.start()
    reduce_all(net, scratch, 1.0 / P)
    keep_right = pltpu.make_async_copy(scratch[1], right_out, out_sem.at[1])
    keep_right.start()
    keep_left.wait()
    keep_right.wait()
    lane.close()


def back(mean, inverse, kept):
    parts, shards = lax.axis_size("rep"), lax.axis_size("rows")
    levels = parts // 2
    _, rows, cols = kept.shape
    width = mean.shape[1]
    piece = cols // (shards * parts)
    anywhere = pl.BlockSpec(memory_space=pl.ANY)
    inside = pl.BlockSpec(memory_space=pltpu.VMEM)
    return pl.pallas_call(
        functools.partial(back_kernel, parts, shards, 256),
        out_shape=[
            jax.ShapeDtypeStruct((parts, rows, width), BF16),
            jax.ShapeDtypeStruct((shards * parts, piece, width), BF16),
        ],
        in_specs=[inside, inside, anywhere],
        out_specs=[anywhere, anywhere],
        scratch_shapes=[
            pltpu.VMEM((parts, rows, cols), BF16),
            pltpu.VMEM((parts, rows, width), BF16),
            pltpu.VMEM((cols, width), F32),
            pltpu.SemaphoreType.DMA((parts,)),
            pltpu.SemaphoreType.DMA((2,)),
            pltpu.SemaphoreType.DMA((2 * levels,)),
            pltpu.SemaphoreType.DMA((2 * levels,)),
        ] + reduce_scratch(parts, shards, piece, width, BF16),
        compiler_params=pltpu.CompilerParams(collective_id=2, has_side_effects=True, vmem_limit_bytes=60 * 1024 * 1024),
        name="back",
    )(mean, inverse, kept)


def final_kernel(scale, left, right, weights, momentum, gradient, weights_out, momentum_out, right_out, turned, normed):
    share = right_out.shape[0]

    @pl.when(pl.program_id(0) == 0)
    def _():
        mean = right[...].astype(F32)
        length = jnp.sqrt(jnp.mean(mean * mean, axis=0, keepdims=True) + tiny)
        turned[...] = right[...].T
        normed[...] = (mean / length).astype(BF16).T
        at = pl.ds(pl.multiple_of(lax.axis_index("rows") * share, share), share)
        right_out[...] = right[at, :].astype(F32) / length

    feedback = jnp.dot(left[...], turned[...], preferred_element_type=F32)
    momentum_out[...] = momentum[...] + gradient[...].astype(F32) - momentum_keep * feedback
    update = jnp.dot(left[...], normed[...], preferred_element_type=F32)
    weights_out[...] = (weights[...].astype(F32) - scale * update).astype(BF16)


def final(left, right, weights, momentum, gradient):
    rows, cols = weights.shape
    width = right.shape[1]
    share = cols // lax.axis_size("rows")
    tile = next(t for t in (256, 224, 128, 64, 32, 16, 8) if rows % t == 0)
    scale = learn_rate * math.sqrt(M / N)

    def streamed(columns):
        return pl.BlockSpec((tile, columns), lambda i: (i, 0))

    def fixed(shape):
        return pl.BlockSpec(shape, lambda i: (0, 0))

    return pl.pallas_call(
        functools.partial(final_kernel, scale),
        grid=(rows // tile,),
        out_shape=[
            jax.ShapeDtypeStruct((rows, cols), BF16),
            jax.ShapeDtypeStruct((rows, cols), F32),
            jax.ShapeDtypeStruct((share, width), F32),
        ],
        in_specs=[streamed(width), fixed((cols, width)), streamed(cols), streamed(cols), streamed(cols)],
        out_specs=[streamed(cols), streamed(cols), fixed((share, width))],
        scratch_shapes=[pltpu.VMEM((width, cols), BF16), pltpu.VMEM((width, cols), BF16)],
        compiler_params=pltpu.CompilerParams(vmem_limit_bytes=60 * 1024 * 1024),
        name="final",
    )(left, right, weights, momentum, gradient)


def per_device(weights, momentum, gradient, right_factor):
    kept, mean, gram = front(momentum, gradient, right_factor)
    width = right_factor.shape[1]
    inverse = inverse_factor(gram.reshape(-1, gram.shape[2]), width)
    left_parts, right_parts = back(mean, inverse, kept)
    left_half = left_parts.reshape(weights.shape[0], width)
    right_half = right_parts.reshape(weights.shape[1], width)
    new_weights, new_momentum, new_right = final(left_half, right_half, weights, momentum[0], gradient[0])
    return (new_weights, new_momentum[None], new_right)


def solution(mesh):
    in_specs = (P("rows", None), P("rep", "rows", None), P("rep", "rows", None), P("rows", None))
    out_specs = (P("rows", None), P("rep", "rows", None), P("rows", None))
    return jax.shard_map(
        per_device, mesh=mesh, in_specs=in_specs, out_specs=out_specs, check_vma=False
    )
```
